32 devices in a mesh: kz: 8 (over z, x), en: 4 (over y, core).
Axes of the slice: x: 2, y: 2, z: 4, core: 2. Of those that a mesh axis runs over, the one named last changes fastest.
Arguments:
- green_real: bfloat16 [8, 96, 128, 128], P('kz', 'en'), may hold values from -6 to 6
- green_imag: bfloat16 [8, 96, 128, 128], P('kz', 'en'), may hold values from -6 to 6
- coupling: bfloat16 [2, 4, 8, 128, 128], P(None, None, 'kz'), may hold values from -0.5 to 0.5
- strengths: float32 [2, 4, 8], replicated, may hold values from 0.1 to 1
- offsets: int32 [2, 8], replicated, may hold values from -4 to 4, as said below
Outputs:
- dressed_real: bfloat16 [8, 96, 128, 128], P('kz', 'en')
- dressed_imag: bfloat16 [8, 96, 128, 128], P('kz', 'en')
The draws below stay inside these ranges and needn't reach their ends.
Inputs may be any that keep to these rules, and one draw needn't show every extreme that they name: Each row of offsets holds each of -4 to -1 and 1 to 4 exactly once.
All inputs are finite; a program needn't handle non-finite values.
Results may differ from the reference program's by a relative error of at most 0.007.
Values may be sent and summed in bfloat16 or wider, within the bound.
A program may use at most 128 MiB of HBM per device.

```python
import math
import jax
import jax.numpy as jnp
from jax import lax

NO = 128
REACH = 4
HOPS = 2
BRANCHES = 4
OFFS = 8
NK = 8
NE = 96


def draw_offsets(key, part):
    base_list = jnp.concatenate([jnp.arange(-REACH, 0), jnp.arange(1, REACH + 1)]).astype(jnp.int32)
    key_list = jax.random.split(key, HOPS)
    rows_list = [jax.random.permutation(key_list[hop_index], base_list) for hop_index in range(HOPS)]
    return jnp.stack(rows_list).astype(jnp.int32)


def steps_of(key, dims, shards, least, largest):
    gain, own = 1.0, jax.random.fold_in(key, 6)
    for dim, parts in shards:
        draws = jnp.exp(jax.random.uniform(jax.random.fold_in(own, dim), (parts,), jnp.float32, least / len(shards), largest / len(shards)))
        gain = gain * jnp.repeat(draws, dims[dim] // parts).reshape([-1 if axis == dim else 1 for axis in range(len(dims))])
    return gain


def noise(own_key, extent, spread, bound, pieces=(), dtype=jnp.bfloat16):
    factor_of = steps_of(own_key, extent, pieces, -0.22, 0.18) if pieces else 1.0
    result = jax.random.normal(own_key, extent, jnp.float32) * spread * factor_of
    return jnp.minimum(jnp.maximum(result, -bound), bound).astype(dtype)


def setup_inputs(seed: int = 0) -> dict:
    splits = jax.random.split(jax.random.key(seed), 6)
    green_real = noise(splits[0], (NK, NE, NO, NO), 1.0, 6.0, ((0, 8), (1, 4)))
    green_imag = noise(splits[1], (NK, NE, NO, NO), 1.0, 6.0, ((0, 8), (1, 4)))
    coupling = noise(splits[2], (HOPS, BRANCHES, NK, NO, NO), NO ** -0.5, 0.5, ((2, 8),))
    strengths = jnp.clip(jnp.exp(jax.random.uniform(splits[3], (HOPS, BRANCHES, OFFS), jnp.float32, math.log(0.1), math.log(1.0))), 0.1, 1.0)
    offsets = draw_offsets(jax.random.fold_in(splits[5], 71), 0)
    return dict(green_real=green_real, green_imag=green_imag, coupling=coupling, strengths=strengths, offsets=offsets)


def reference(green_real, green_imag, coupling, strengths, offsets):
    stacked = jnp.stack([green_real, green_imag], axis=1)
    levels = jnp.arange(-REACH, REACH + 1).astype(jnp.int32)
    match_table = (offsets[:, None, :, None] == levels[None, None, None, :]).astype(jnp.float32)
    weights_table = jnp.sum(strengths[:, :, :, None] * match_table, axis=2)

    def per_momentum(momentum):
        own_block = lax.dynamic_index_in_dim(stacked, momentum, 0, keepdims=False).astype(jnp.float32)
        self_energy = jnp.zeros(own_block.shape, jnp.float32)
        for hop_index in range(HOPS):
            source = lax.dynamic_index_in_dim(stacked, ((momentum - hop_index - 1) % NK).astype(jnp.int32), 0, keepdims=False).astype(jnp.float32)
            padded = jnp.pad(source, ((0, 0), (REACH, REACH), (0, 0), (0, 0)))
            for branch_index in range(BRANCHES):
                summed_block = jnp.zeros(own_block.shape, jnp.float32)
                for step_index in range(2 * REACH + 1):
                    energy_shift = step_index - REACH
                    if energy_shift == 0:
                        continue
                    summed_block = summed_block + weights_table[hop_index, branch_index, step_index] * padded[:, REACH - energy_shift:REACH - energy_shift + NE]
                summed_block = lax.optimization_barrier(summed_block.astype(jnp.bfloat16)).astype(jnp.float32)
                matrix = lax.dynamic_index_in_dim(coupling[hop_index, branch_index], momentum, 0, keepdims=False).astype(jnp.float32)
                left_prod = jnp.einsum("ab,xebc->xeac", matrix, summed_block)
                left_prod = lax.optimization_barrier(left_prod.astype(jnp.bfloat16)).astype(jnp.float32)
                self_energy = self_energy + jnp.einsum("xeab,cb->xeac", left_prod, matrix)
        self_energy = lax.optimization_barrier(self_energy.astype(jnp.bfloat16)).astype(jnp.float32)
        real_part = own_block[0]
        imag_part = own_block[1]
        self_real = self_energy[0]
        self_imag = self_energy[1]
        prod_real = jnp.einsum("eab,ebc->eac", real_part, self_real) - jnp.einsum("eab,ebc->eac", imag_part, self_imag)
        prod_imag = jnp.einsum("eab,ebc->eac", real_part, self_imag) + jnp.einsum("eab,ebc->eac", imag_part, self_real)
        prod_real = lax.optimization_barrier(prod_real.astype(jnp.bfloat16)).astype(jnp.float32)
        prod_imag = lax.optimization_barrier(prod_imag.astype(jnp.bfloat16)).astype(jnp.float32)
        back_real = jnp.einsum("eab,ebc->eac", prod_real, real_part) - jnp.einsum("eab,ebc->eac", prod_imag, imag_part)
        back_imag = jnp.einsum("eab,ebc->eac", prod_real, imag_part) + jnp.einsum("eab,ebc->eac", prod_imag, real_part)
        dressed_real = (real_part + back_real / NO).astype(jnp.bfloat16)
        dressed_imag = (imag_part + back_imag / NO).astype(jnp.bfloat16)
        return jnp.stack([dressed_real, dressed_imag])

    results = lax.map(per_momentum, jnp.arange(NK).astype(jnp.int32))
    return (results[:, 0], results[:, 1])
```

```python
import functools

import jax
import jax.numpy as jnp
from jax import lax
from jax.experimental import pallas as pl
from jax.experimental.pallas import tpu as pltpu
from jax.sharding import PartitionSpec as P

REACH = 4
TAPS = 2 * REACH + 1
TILE = 64
LANES = 16
SINGLES = REACH + 2
MESH = pl.DeviceIdType.MESH
GRANT = 60 * 2**20


def pieces_of(energies):
    pieces = [(energies - 4, 1), (energies - 3, 1), (energies - 2, 2), (0, 2), (2, 2)]
    edges = len(pieces)
    start, last = REACH, energies - REACH
    while start < last:
        size = 2 if last - start >= SINGLES + 2 else 1
        pieces.append((start, size))
        start += size
    return pieces, edges


def kernel(counts, real_hbm, imag_hbm, coupling_hbm, strengths_hbm, offsets_hbm, real_out, imag_out,
           own, near, far, coupling, strengths, offsets, turned, flat, weights, summed, sigma, partial, rotated, dressed,
           own_sem, small_sem, out_sem, far_send, far_recv, near_send, near_recv, halo_send, halo_recv, ack):
    momenta, sections = counts
    hops, branches, orbitals = coupling.shape[0], coupling.shape[1], coupling.shape[-1]
    energies = own.shape[1]
    pieces, edges = pieces_of(energies)
    kz, en = lax.axis_index("kz"), lax.axis_index("en")
    odd = lax.rem(kz, 2)
    even = 1 - odd
    partner = kz + 1 - 2 * odd
    ahead, behind = lax.rem(kz + 2, momenta), lax.rem(kz + momenta - 2, momenta)
    has_low, has_high = en > 0, en < sections - 1
    sources, outs, fields = (real_hbm, imag_hbm), (real_out, imag_out), (near, far)

    barrier = pltpu.get_barrier_semaphore()
    pl.semaphore_signal(barrier, inc=1, device_id=(behind, en), device_id_type=MESH)

    @pl.when(even == 1)
    def _():
        pl.semaphore_signal(barrier, inc=1, device_id=(partner, en), device_id_type=MESH)

    @pl.when(has_high)
    def _():
        pl.semaphore_signal(barrier, inc=1, device_id=(kz, en + 1), device_id_type=MESH)

    smalls = [pltpu.make_async_copy(a, b, small_sem.at[i]) for i, (a, b) in enumerate(
        ((coupling_hbm, coupling), (strengths_hbm, strengths), (offsets_hbm, offsets)))]
    for copy in smalls:
        copy.start()
    pl.semaphore_wait(barrier, 1 + odd + has_low.astype(jnp.int32))

    def far_copy(piece, start, size, part):
        return pltpu.make_async_remote_copy(
            sources[part].at[0, pl.ds(start, size)], far.at[part, pl.ds(REACH + start, size)],
            far_send.at[piece, part], far_recv.at[piece, part], device_id=(ahead, en), device_id_type=MESH)

    def near_copy(piece, start, size, part, relay):
        rows = pl.ds(REACH + start, size)
        source = far.at[part, rows] if relay else sources[part].at[0, pl.ds(start, size)]
        return pltpu.make_async_remote_copy(
            source, near.at[part, rows],
            near_send.at[piece, part], near_recv.at[piece, part], device_id=(partner, en), device_id_type=MESH)

    def halo_copy(hop, side):
        field = fields[hop]
        if side == 0:
            source, target, to = energies, 0, lax.rem(en + 1, sections)
        else:
            source, target, to = REACH, REACH + energies, lax.rem(en + sections - 1, sections)
        return pltpu.make_async_remote_copy(
            field.at[:, pl.ds(source, REACH)], field.at[:, pl.ds(target, REACH)],
            halo_send.at[hop, side], halo_recv.at[hop, side], device_id=(kz, to), device_id_type=MESH)

    for piece, (start, size) in enumerate(pieces):
        for part in range(2):
            far_copy(piece, start, size, part).start()

    @pl.when(odd == 1)
    def _():
        pl.semaphore_signal(ack.at[0], inc=1, device_id=(partner, en), device_id_type=MESH)

    @pl.when(has_low)
    def _():
        pl.semaphore_signal(ack.at[1], inc=1, device_id=(kz, en - 1), device_id_type=MESH)

    @pl.when(odd == 0)
    def _():
        pl.semaphore_wait(ack.at[0], 1)
        for piece, (start, size) in enumerate(pieces):
            for part in range(2):
                near_copy(piece, start, size, part, False).start()

    owns = [pltpu.make_async_copy(sources[part].at[0], own.at[part], own_sem.at[part]) for part in range(2)]
    for copy in owns:
        copy.start()

    @pl.when(has_high)
    def _():
        pl.semaphore_wait(ack.at[1], 1)

    def arrive(piece, start, size):
        for part in range(2):
            far_copy(piece, start, size, part).wait_recv()

            @pl.when(odd == 1)
            def _(part=part):
                near_copy(piece, start, size, part, True).start()
        for part in range(2):
            near_copy(piece, start, size, part, False).wait_recv()

    zeros = jnp.zeros((2, REACH, orbitals, orbitals), jnp.bfloat16)
    blank = jnp.zeros((orbitals, orbitals), jnp.bfloat16)

    @pl.when(en == 0)
    def _():
        near[:, pl.ds(0, REACH)] = zeros
        far[:, pl.ds(0, REACH)] = zeros

    @pl.when(en == sections - 1)
    def _():
        near[:, pl.ds(REACH + energies, REACH)] = zeros
        far[:, pl.ds(REACH + energies, REACH)] = zeros

    def place_of(hop, branch):
        return hop * branches + branch

    def prepare(hop, branch):
        matrix = coupling[hop, branch, 0].astype(jnp.float32)
        turned[hop, branch] = matrix.T.astype(jnp.bfloat16)
        flat[place_of(hop, branch)] = (matrix * (1.0 / orbitals)).astype(jnp.bfloat16)
        for tap in range(TAPS):
            if tap == REACH:
                continue
            total = jnp.float32(0)
            for index in range(offsets.shape[1]):
                total = total + jnp.where(
                    offsets[hop, index] == REACH - tap, strengths[hop, branch, index], 0.0)
            weights[place_of(hop, branch) * TAPS + tap] = jnp.full(
                (LANES, orbitals), total, jnp.float32).astype(jnp.bfloat16)

    def scale_of(hop, branch, tap, rows):
        return jnp.concatenate([weights[place_of(hop, branch) * TAPS + tap]] * (rows // LANES), axis=0)

    def mix(energy, slot, hop, part, row, taps):
        field = fields[hop]
        sums = [None] * branches
        for pair in range(0, len(taps), 2):
            some = taps[pair:pair + 2]
            windows = [field[part, energy + tap, row:row + TILE, :] for tap in some]
            for branch in range(branches):
                terms = [scale_of(hop, branch, tap, TILE) * window for tap, window in zip(some, windows)]
                term = terms[0] if len(terms) == 1 else terms[0] + terms[1]
                sums[branch] = term if sums[branch] is None else sums[branch] + term
        for branch in range(branches):
            summed[slot, hop, branch, part * orbitals + row:part * orbitals + row + TILE, :] = sums[branch]

    every = [tap for tap in range(TAPS) if tap != REACH]
    units = [(part, row) for part in range(2) for row in range(0, orbitals, TILE)]
    share = -(-2 * len(units) // branches)

    def right(slot, hop, pair):
        first, second = 2 * pair, 2 * pair + 1
        both = jnp.concatenate([summed[slot, hop, first], summed[slot, hop, second]], axis=1)
        blocks = jnp.concatenate([jnp.concatenate([turned[hop, first], blank], axis=1),
                                  jnp.concatenate([blank, turned[hop, second]], axis=1)], axis=0)
        both = jnp.dot(both, blocks, preferred_element_type=jnp.float32).astype(jnp.bfloat16)
        return [jnp.concatenate([both[:orbitals, side:side + orbitals], both[orbitals:, side:side + orbitals]], axis=1)
                for side in (0, orbitals)]

    def left(parts):
        total = jnp.dot(jnp.concatenate([flat[place] for place in range(hops * branches)], axis=1),
                        jnp.concatenate(parts, axis=0), preferred_element_type=jnp.float32).astype(jnp.bfloat16)
        return total[:, :orbitals], total[:, orbitals:]

    def paired(real, imag):
        return jnp.concatenate(
            [jnp.concatenate([real, imag], axis=1), jnp.concatenate([-imag, real], axis=1)], axis=0)

    def product(energy, real, imag):
        return jnp.dot(jnp.concatenate([own[0, energy], own[1, energy]], axis=1), paired(real, imag),
                       preferred_element_type=jnp.float32).astype(jnp.bfloat16)

    def dress(energy, prod):
        real, imag = own[0, energy], own[1, energy]
        back = jnp.dot(prod, paired(real, imag), preferred_element_type=jnp.float32)
        dressed[0, energy] = (real.astype(jnp.float32) + back[:, :orbitals]).astype(jnp.bfloat16)
        dressed[1, energy] = (imag.astype(jnp.float32) + back[:, orbitals:]).astype(jnp.bfloat16)

    def stage(mixing, lefting, dressing):
        prod = None
        if dressing is not None:
            prod = product(dressing[0], sigma[dressing[1], 0], sigma[dressing[1], 1])
        parts = []
        for hop in range(hops):
            for pair in range(branches // 2):
                if lefting is not None:
                    parts += right(lefting[1], hop, pair)
                if mixing is not None:
                    for part, row in units[pair * share:(pair + 1) * share]:
                        mix(mixing[0], mixing[1], hop, part, row, every)
            if hop == 0 and prod is not None:
                dress(dressing[0], prod)
        if lefting is not None:
            real, imag = left(parts)
            sigma[lefting[1], 0], sigma[lefting[1], 1] = real, imag

    last = energies - REACH - 1
    tail = [e for e in range(last - REACH, energies) if e != last]

    def begin(energy, until, slot):
        taps = [tap for tap in every if not until < energy + tap - REACH <= last]
        for hop in range(hops):
            for part, row in units:
                mix(energy, slot, hop, part, row, taps)
        for hop in range(hops):
            for pair in range(branches // 2):
                for branch, value in zip((2 * pair, 2 * pair + 1), right(slot, hop, pair)):
                    for part in range(2):
                        partial[tail.index(energy), place_of(hop, branch), part] = (
                            value[:, part * orbitals:(part + 1) * orbitals])

    def rotate(source, hop):
        rows = jnp.concatenate([fields[hop][0, REACH + source], fields[hop][1, REACH + source]], axis=0)
        for pair in range(branches // 2):
            first, second = 2 * pair, 2 * pair + 1
            both = jnp.dot(rows, jnp.concatenate([turned[hop, first], turned[hop, second]], axis=1),
                           preferred_element_type=jnp.float32).astype(jnp.bfloat16)
            for index, branch in enumerate((first, second)):
                for part in range(2):
                    rotated[source % 2, place_of(hop, branch), part] = both[
                        part * orbitals:(part + 1) * orbitals, index * orbitals:(index + 1) * orbitals]

    def updated(energy, source, hop, branch, part):
        place = place_of(hop, branch)
        return (partial[tail.index(energy), place, part]
                + scale_of(hop, branch, source - energy + REACH, orbitals) * rotated[source % 2, place, part])

    def update(energy, source):
        for hop in range(hops):
            for branch in range(branches):
                for part in range(2):
                    partial[tail.index(energy), place_of(hop, branch), part] = updated(energy, source, hop, branch, part)

    def out_copy(index, start, size, part):
        return pltpu.make_async_copy(dressed.at[part, pl.ds(start, size)], outs[part].at[0, pl.ds(start, size)],
                                     out_sem.at[index, part])

    def out(start, size):
        for part in range(2):
            out_copy(start, start, size, part).start()

    def halo_out(hop, side, cond):
        @pl.when(cond)
        def _():
            halo_copy(hop, side).start()

    def halo_in(side, cond):
        @pl.when(cond)
        def _():
            for hop in range(hops):
                halo_copy(hop, side).wait_recv()

    jobs = [(hop, branch) for hop in range(hops) for branch in range(branches)]
    for piece in range(edges):
        arrive(piece, *pieces[piece])
        if piece == 2:
            for hop in range(hops):
                halo_out(hop, 0, has_high)
        if piece == edges - 1:
            for hop in range(hops):
                halo_out(hop, 1, has_low)
        if piece == 0:
            for copy in smalls:
                copy.wait()
        for job in jobs[piece * 2:piece * 2 + 2]:
            prepare(*job)
    for copy in owns:
        copy.wait()

    piece, start = edges, REACH
    stages = 0

    def step(energy):
        stage((energy, energy % 2), (energy - 1, (energy - 1) % 2) if energy > 0 else None,
              (energy - 2, energy % 2) if energy > 1 else None)

    halo_in(0, has_low)
    arrive(piece, *pieces[piece])
    for energy in range(pieces[piece][1]):
        step(energy)
        stages += 1
    start, piece = start + pieces[piece][1], piece + 1
    halo_in(1, has_high)
    for index, energy in enumerate(range(last + 1, energies)):
        begin(energy, last - REACH, 2 + index % 2)
    if stages == 1:
        arrive(piece, *pieces[piece])
        for energy in range(stages, stages + pieces[piece][1]):
            step(energy)
        stages += pieces[piece][1]
        start, piece = start + pieces[piece][1], piece + 1

    pairs = sum(size == 2 for _, size in pieces[piece:])
    base_piece, base_start, parity = piece, start, stages % 2

    def body(index, carry):
        first = base_start + 2 * index
        arrive(base_piece + index, first, 2)
        for offset in range(2):
            energy, slot = first - REACH + offset, (parity + offset) % 2
            stage((energy, slot), (energy - 1, 1 - slot), (energy - 2, slot))
        for part in range(2):
            out_copy(first - REACH - 2, first - REACH - 2, 2, part).start()
        return carry

    lax.fori_loop(0, pairs, body, 0)
    outs_started = [(stages - 2 + 2 * index, 2) for index in range(pairs)]
    piece, start, stages = piece + pairs, start + 2 * pairs, stages + 2 * pairs

    def late(source):
        for hop in range(hops):
            rotate(source, hop)
        for energy in tail:
            ready = last - REACH if energy > last else energy - 1
            if energy != source and abs(energy - source) <= REACH and source > ready:
                update(energy, source)

    for source in range(start, last):
        arrive(piece, source, 1)
        step(stages)
        opened = source + 1
        if last - REACH <= opened < last:
            begin(opened, source, 2)
        if source > last - REACH:
            late(source)
        out(stages - 2, 1)
        outs_started.append((stages - 2, 1))
        stages += 1
        piece += 1
    before = stages - 1
    stage((last, stages % 2), (before, before % 2), (before - 1, (before - 1) % 2))
    out(before - 1, 1)
    stage(None, (last, stages % 2), (before, before % 2))
    out(before, 1)
    outs_started += [(before - 1, 1), (before, 1)]

    def sends(wanted):
        for index in wanted:
            for part in range(2):
                far_copy(index, *pieces[index], part).wait_send()
                near_copy(index, *pieces[index], part, False).wait_send()

    arrive(piece, last, 1)
    for hop in range(hops):
        rotate(last, hop)
    waiting = [(last, product(last, sigma[stages % 2, 0], sigma[stages % 2, 1]))]
    sums = []
    for energy in tail + [None, None]:
        made = None
        if energy is not None:
            parts = [jnp.concatenate([updated(energy, last, hop, branch, part) for part in range(2)], axis=1)
                     for hop, branch in jobs]
            made = (energy, *left(parts))
        ready = waiting.pop(0) if waiting else None
        if sums:
            done = sums.pop(0)
            waiting.append((done[0], product(*done)))
        if made is not None:
            sums.append(made)
        if ready is not None:
            dress(*ready)
            out(ready[0], 1)
            outs_started.append((ready[0], 1))
    for ready in waiting:
        dress(*ready)
        out(ready[0], 1)
        outs_started.append((ready[0], 1))

    sends(range(len(pieces)))
    for side, cond in ((0, has_high), (1, has_low)):
        @pl.when(cond)
        def _(side=side):
            for hop in range(hops):
                halo_copy(hop, side).wait_send()
    for first, size in outs_started:
        for part in range(2):
            out_copy(first, first, size, part).wait()


def deliver(real_in, imag_in, real_out, imag_out, held, in_sem, out_sem):
    chunks = held.shape[1]
    size = held.shape[2]
    refs = ((real_in, real_out), (imag_in, imag_out))

    def fetch(part, chunk):
        return pltpu.make_async_copy(
            refs[part][0].at[0, pl.ds(chunk * size, size)], held.at[part, chunk], in_sem.at[part, chunk])

    def store(part, chunk):
        return pltpu.make_async_copy(
            held.at[part, chunk], refs[part][1].at[0, pl.ds(chunk * size, size)], out_sem.at[part, chunk])

    order = [(part, chunk) for chunk in range(chunks) for part in range(2)]
    for key in order:
        fetch(*key).start()
    for key in order:
        fetch(*key).wait()
        store(*key).start()
    for key in order:
        store(*key).wait()


def shards(counts, green_real, green_imag, coupling, strengths, offsets):
    energies, orbitals = green_real.shape[1], green_real.shape[2]
    hops, branches = coupling.shape[0], coupling.shape[1]
    pieces, _ = pieces_of(energies)
    anywhere = pl.BlockSpec(memory_space=pl.ANY)
    dma = pltpu.SemaphoreType.DMA
    chunks = len(pieces)
    square = (orbitals, orbitals)
    extended = (2, energies + 2 * REACH) + square
    shapes = [jax.ShapeDtypeStruct(green_real.shape, jnp.bfloat16)] * 2
    dressed = pl.pallas_call(
        functools.partial(kernel, counts),
        out_shape=shapes,
        in_specs=[anywhere] * 5,
        out_specs=[anywhere] * 2,
        scratch_shapes=[
            pltpu.VMEM((2, energies) + square, jnp.bfloat16),
            pltpu.VMEM(extended, jnp.bfloat16),
            pltpu.VMEM(extended, jnp.bfloat16),
            pltpu.VMEM(coupling.shape, jnp.bfloat16),
            pltpu.SMEM(strengths.shape, jnp.float32),
            pltpu.SMEM(offsets.shape, jnp.int32),
            pltpu.VMEM((hops, branches) + square, jnp.bfloat16),
            pltpu.VMEM((hops * branches,) + square, jnp.bfloat16),
            pltpu.VMEM((hops * branches * TAPS, LANES, orbitals), jnp.bfloat16),
            pltpu.VMEM((4, hops, branches, 2 * orbitals, orbitals), jnp.bfloat16),
            pltpu.VMEM((2, 2) + square, jnp.bfloat16),
            pltpu.VMEM((2 * REACH, hops * branches, 2) + square, jnp.bfloat16),
            pltpu.VMEM((2, hops * branches, 2) + square, jnp.bfloat16),
            pltpu.VMEM((2, energies) + square, jnp.bfloat16),
            dma((2,)), dma((3,)), dma((energies, 2)),
            dma((chunks, 2)), dma((chunks, 2)),
            dma((chunks, 2)), dma((chunks, 2)),
            dma((hops, 2)), dma((hops, 2)),
            pltpu.SemaphoreType.REGULAR((2,)),
        ],
        compiler_params=pltpu.CompilerParams(
            collective_id=0, has_side_effects=True, vmem_limit_bytes=GRANT),
    )(green_real, green_imag, coupling, strengths, offsets)
    parts = 3 if energies % 3 == 0 else 1
    return pl.pallas_call(
        deliver,
        out_shape=shapes,
        in_specs=[anywhere] * 2,
        out_specs=[anywhere] * 2,
        scratch_shapes=[
            pltpu.VMEM((2, parts, energies // parts) + square, jnp.bfloat16),
            dma((2, parts)), dma((2, parts)),
        ],
        compiler_params=pltpu.CompilerParams(vmem_limit_bytes=GRANT),
    )(*dressed)


def solution(mesh):
    blocks = P("kz", "en", None, None)
    counts = (mesh.shape["kz"], mesh.shape["en"])
    return jax.shard_map(
        functools.partial(shards, counts), mesh=mesh,
        in_specs=(blocks, blocks, P(None, None, "kz", None, None), P(), P()),
        out_specs=(blocks, blocks), check_vma=False)
```

```python
import functools

import jax
import jax.numpy as jnp
from jax import lax
from jax.experimental import pallas as pl
from jax.experimental.pallas import tpu as pltpu
from jax.sharding import PartitionSpec as P

REACH = 4
TAPS = 2 * REACH + 1
TILE = 64
LANES = 16
MESH = pl.DeviceIdType.MESH
GRANT = 60 * 2**20


def pieces_of(energies):
    order = list(range(energies - REACH, energies)) + list(range(energies - REACH))
    pieces = [(energy, 1) for energy in order]
    edges = 2 * REACH
    return pieces, edges


def kernel(counts, real_hbm, imag_hbm, coupling_hbm, strengths_hbm, offsets_hbm, real_out, imag_out,
           own, near, far, coupling, strengths, offsets, turned, flat, weights, sigma, partial, rotated, dressed,
           own_sem, small_sem, out_sem, far_send, far_recv, near_send, near_recv, halo_send, halo_recv, ack):
    momenta, sections = counts
    hops, branches, orbitals = coupling.shape[0], coupling.shape[1], coupling.shape[-1]
    energies = own.shape[1]
    pieces, edges = pieces_of(energies)
    kz, en = lax.axis_index("kz"), lax.axis_index("en")
    odd = lax.rem(kz, 2)
    even = 1 - odd
    partner = kz + 1 - 2 * odd
    ahead, behind = lax.rem(kz + 2, momenta), lax.rem(kz + momenta - 2, momenta)
    has_low, has_high = en > 0, en < sections - 1
    sources, outs, fields = (real_hbm, imag_hbm), (real_out, imag_out), (near, far)

    barrier = pltpu.get_barrier_semaphore()
    pl.semaphore_signal(barrier, inc=1, device_id=(behind, en), device_id_type=MESH)

    @pl.when(even == 1)
    def _():
        pl.semaphore_signal(barrier, inc=1, device_id=(partner, en), device_id_type=MESH)

    @pl.when(has_high)
    def _():
        pl.semaphore_signal(barrier, inc=1, device_id=(kz, en + 1), device_id_type=MESH)

    smalls = [pltpu.make_async_copy(a, b, small_sem.at[i]) for i, (a, b) in enumerate(
        ((coupling_hbm, coupling), (strengths_hbm, strengths), (offsets_hbm, offsets)))]
    for copy in smalls:
        copy.start()
    pl.semaphore_wait(barrier, 1 + odd + has_low.astype(jnp.int32))

    def far_copy(piece, start, size, part):
        return pltpu.make_async_remote_copy(
            sources[part].at[0, pl.ds(start, size)], far.at[part, pl.ds(REACH + start, size)],
            far_send.at[part], far_recv.at[piece, part], device_id=(ahead, en), device_id_type=MESH)

    def near_copy(piece, start, size, part, relay):
        rows = pl.ds(REACH + start, size)
        source = far.at[part, rows] if relay else sources[part].at[0, pl.ds(start, size)]
        return pltpu.make_async_remote_copy(
            source, near.at[part, rows],
            near_send.at[part], near_recv.at[piece], device_id=(partner, en), device_id_type=MESH)

    def halo_copy(hop, side):
        field = fields[hop]
        if side == 0:
            source, target, to = energies, 0, lax.rem(en + 1, sections)
        else:
            source, target, to = REACH, REACH + energies, lax.rem(en + sections - 1, sections)
        return pltpu.make_async_remote_copy(
            field.at[:, pl.ds(source, REACH)], field.at[:, pl.ds(target, REACH)],
            halo_send.at[hop, side], halo_recv.at[hop, side], device_id=(kz, to), device_id_type=MESH)

    @pl.when(odd == 1)
    def _():
        pl.semaphore_signal(ack.at[0], inc=1, device_id=(partner, en), device_id_type=MESH)

    @pl.when(has_low)
    def _():
        pl.semaphore_signal(ack.at[1], inc=1, device_id=(kz, en - 1), device_id_type=MESH)

    def send_far(first, stop):
        for piece in range(first, stop):
            for part in range(2):
                far_copy(piece, *pieces[piece], part).start()

    def send_near(first, stop):
        @pl.when(odd == 0)
        def _():
            if first == 0:
                pl.semaphore_wait(ack.at[0], 1)
            for piece in range(first, stop):
                for part in range(2):
                    near_copy(piece, *pieces[piece], part, False).start()

    send_far(0, edges)
    send_near(0, edges)
    send_far(edges, len(pieces))
    send_near(edges, len(pieces))

    owns = [pltpu.make_async_copy(sources[part].at[0], own.at[part], own_sem.at[part]) for part in range(2)]
    for copy in owns:
        copy.start()

    @pl.when(has_high)
    def _():
        pl.semaphore_wait(ack.at[1], 1)

    def arrive(piece, start, size):
        for part in range(2):
            far_copy(piece, start, size, part).wait_recv()

            @pl.when(odd == 1)
            def _(part=part):
                near_copy(piece, start, size, part, True).start()
        rows = pl.ds(REACH + start, size)
        pltpu.make_async_copy(near.at[:, rows], near.at[:, rows], near_recv.at[piece]).wait()

    zeros = jnp.zeros((2, REACH, orbitals, orbitals), jnp.bfloat16)
    blank = jnp.zeros((orbitals, orbitals), jnp.bfloat16)

    @pl.when(en == 0)
    def _():
        near[:, pl.ds(0, REACH)] = zeros
        far[:, pl.ds(0, REACH)] = zeros

    @pl.when(en == sections - 1)
    def _():
        near[:, pl.ds(REACH + energies, REACH)] = zeros
        far[:, pl.ds(REACH + energies, REACH)] = zeros

    def place_of(hop, branch):
        return hop * branches + branch

    def prepare(hop, branch):
        matrix = coupling[hop, branch, 0].astype(jnp.float32)
        turned[hop, branch] = matrix.T.astype(jnp.bfloat16)
        flat[place_of(hop, branch)] = (matrix * (1.0 / orbitals)).astype(jnp.bfloat16)
        for tap in range(TAPS):
            if tap == REACH:
                continue
            total = jnp.float32(0)
            for index in range(offsets.shape[1]):
                total = total + jnp.where(
                    offsets[hop, index] == REACH - tap, strengths[hop, branch, index], 0.0)
            weights[place_of(hop, branch) * TAPS + tap] = jnp.full(
                (LANES, orbitals), total, jnp.float32).astype(jnp.bfloat16)

    def scale_of(hop, branch, tap, rows):
        return jnp.concatenate([weights[place_of(hop, branch) * TAPS + tap]] * (rows // LANES), axis=0)

    every = [tap for tap in range(TAPS) if tap != REACH]

    def right(energy, hop, pair, taps):
        field = fields[hop]
        both = (2 * pair, 2 * pair + 1)
        rows = []
        for part in range(2):
            for row in range(0, orbitals, TILE):
                sums = [None, None]
                for first in range(0, len(taps), 2):
                    some = taps[first:first + 2]
                    windows = [field[part, energy + tap, row:row + TILE, :] for tap in some]
                    for index, branch in enumerate(both):
                        terms = [scale_of(hop, branch, tap, TILE) * window for tap, window in zip(some, windows)]
                        term = terms[0] if len(terms) == 1 else terms[0] + terms[1]
                        sums[index] = term if sums[index] is None else sums[index] + term
                rows.append(jnp.concatenate(sums, axis=1))
        blocks = jnp.concatenate([jnp.concatenate([turned[hop, both[0]], blank], axis=1),
                                  jnp.concatenate([blank, turned[hop, both[1]]], axis=1)], axis=0)
        made = jnp.dot(jnp.concatenate(rows, axis=0), blocks, preferred_element_type=jnp.float32).astype(jnp.bfloat16)
        return [jnp.concatenate([made[:orbitals, side:side + orbitals], made[orbitals:, side:side + orbitals]], axis=1)
                for side in (0, orbitals)]

    def left(parts):
        total = jnp.dot(jnp.concatenate([flat[place] for place in range(hops * branches)], axis=1),
                        jnp.concatenate(parts, axis=0), preferred_element_type=jnp.float32).astype(jnp.bfloat16)
        return total[:, :orbitals], total[:, orbitals:]

    def paired(real, imag):
        return jnp.concatenate(
            [jnp.concatenate([real, imag], axis=1), jnp.concatenate([-imag, real], axis=1)], axis=0)

    def product(energy, real, imag):
        return jnp.dot(jnp.concatenate([own[0, energy], own[1, energy]], axis=1), paired(real, imag),
                       preferred_element_type=jnp.float32).astype(jnp.bfloat16)

    def dress(energy, prod):
        real, imag = own[0, energy], own[1, energy]
        back = jnp.dot(prod, paired(real, imag), preferred_element_type=jnp.float32)
        dressed[0, energy] = (real.astype(jnp.float32) + back[:, :orbitals]).astype(jnp.bfloat16)
        dressed[1, energy] = (imag.astype(jnp.float32) + back[:, orbitals:]).astype(jnp.bfloat16)

    def stage(energy, slot, before):
        if before is not None:
            prod = product(before, sigma[1 - slot, 0], sigma[1 - slot, 1])
        parts = []
        for hop in range(hops):
            for pair in range(branches // 2):
                parts += right(energy, hop, pair, every)
            if hop == 0 and before is not None:
                dress(before, prod)
        sigma[slot, 0], sigma[slot, 1] = left(parts)

    last = energies - REACH - 1
    tail = [e for e in range(last - REACH, energies) if e != last]

    def begin(energy, until):
        taps = [tap for tap in every if not until < energy + tap - REACH <= last]
        for hop in range(hops):
            for pair in range(branches // 2):
                for branch, value in zip((2 * pair, 2 * pair + 1), right(energy, hop, pair, taps)):
                    for part in range(2):
                        partial[tail.index(energy), place_of(hop, branch), part] = (
                            value[:, part * orbitals:(part + 1) * orbitals])

    def ready(energy):
        return last - REACH if energy > last else energy - 1

    def rotate(source, hop):
        rows = jnp.concatenate([fields[hop][0, REACH + source], fields[hop][1, REACH + source]], axis=0)
        for pair in range(branches // 2):
            first, second = 2 * pair, 2 * pair + 1
            both = jnp.dot(rows, jnp.concatenate([turned[hop, first], turned[hop, second]], axis=1),
                           preferred_element_type=jnp.float32).astype(jnp.bfloat16)
            for index, branch in enumerate((first, second)):
                for part in range(2):
                    rotated[last - source, place_of(hop, branch), part] = both[
                        part * orbitals:(part + 1) * orbitals, index * orbitals:(index + 1) * orbitals]

    def updated(energy, hop, branch, part):
        place = place_of(hop, branch)
        total = None
        for source in range(last - REACH + 1, last + 1):
            if source > ready(energy) and source != energy and abs(source - energy) <= REACH:
                term = scale_of(hop, branch, source - energy + REACH, orbitals) * rotated[last - source, place, part]
                total = term if total is None else total + term
        return total + partial[tail.index(energy), place, part]

    def out_copy(start, size, part):
        return pltpu.make_async_copy(
            dressed.at[part, pl.ds(start, size)], outs[part].at[0, pl.ds(start, size)], out_sem.at[part])

    def out(start, size):
        for part in range(2):
            out_copy(start, size, part).start()

    def halo_out(hop, side, cond):
        @pl.when(cond)
        def _():
            halo_copy(hop, side).start()

    def halo_in(side, cond):
        @pl.when(cond)
        def _():
            for hop in range(hops):
                halo_copy(hop, side).wait_recv()

    jobs = [(hop, branch) for hop in range(hops) for branch in range(branches)]
    for piece in range(edges):
        arrive(piece, *pieces[piece])
        if piece == REACH - 1:
            for hop in range(hops):
                halo_out(hop, 0, has_high)
        if piece == edges - 1:
            for hop in range(hops):
                halo_out(hop, 1, has_low)
        if piece == 0:
            for copy in smalls:
                copy.wait()
        for job in jobs[piece::edges]:
            prepare(*job)
    for copy in owns:
        copy.wait()

    piece, start = edges, REACH
    stages = 0

    def step(energy):
        stage(energy, energy % 2, energy - 1 if energy > 0 else None)

    halo_in(0, has_low)
    count = last - 1 - 2 * REACH
    for energy in range(2 - count % 2):
        arrive(piece, *pieces[piece])
        step(energy)
        stages, start, piece = stages + 1, start + 1, piece + 1
    pairs = (count - stages) // 2
    if stages > 1:
        out(0, stages - 1)

    base_piece, base_start, parity = piece, start, stages % 2

    def body(index, carry):
        first = base_start + 2 * index
        for offset in range(2):
            arrive(base_piece + 2 * index + offset, first + offset, 1)
            energy = first - REACH + offset
            stage(energy, (parity + offset) % 2, energy - 1)
        for part in range(2):
            out_copy(first - REACH - 1, 2, part).start()
        return carry

    split = pairs - 1
    lax.fori_loop(0, split, body, 0)
    halo_in(1, has_high)
    upper = list(range(last + 1, energies))
    for energy in upper[:2]:
        begin(energy, last - REACH)
    lax.fori_loop(split, pairs, body, 0)
    for energy in upper[2:]:
        begin(energy, last - REACH)
    piece, start, stages = piece + 2 * pairs, start + 2 * pairs, stages + 2 * pairs

    for source in range(start, last):
        arrive(piece, source, 1)
        step(stages)
        opened = source + 1
        if last - REACH <= opened < last:
            begin(opened, source)
        if source > last - REACH:
            for hop in range(hops):
                rotate(source, hop)
        out(stages - 1, 1)
        stages += 1
        piece += 1
    stage(last, stages % 2, stages - 1)
    out(stages - 1, 1)

    for side, cond in ((0, has_high), (1, has_low)):
        @pl.when(cond)
        def _(side=side):
            for hop in range(hops):
                halo_copy(hop, side).wait_send()
    arrive(piece, last, 1)
    for hop in range(hops):
        rotate(last, hop)
    waiting = [(last, product(last, sigma[stages % 2, 0], sigma[stages % 2, 1]))]
    sums = []
    for energy in tail + [None, None]:
        made = None
        if energy is not None:
            parts = [jnp.concatenate([updated(energy, hop, branch, part) for part in range(2)], axis=1)
                     for hop, branch in jobs]
            made = (energy, *left(parts))
        turn = waiting.pop(0) if waiting else None
        if sums:
            done = sums.pop(0)
            waiting.append((done[0], product(*done)))
        if made is not None:
            sums.append(made)
        if turn is not None:
            dress(*turn)
            out(turn[0], 1)

    for part in range(2):
        far_copy(0, 0, energies, part).wait_send()
        near_copy(0, 0, energies, part, False).wait_send()
        out_copy(0, energies, part).wait()


def deliver(real_in, imag_in, real_out, imag_out, held, in_sem, out_sem):
    chunks = held.shape[1]
    size = held.shape[2]
    refs = ((real_in, real_out), (imag_in, imag_out))

    def fetch(part, chunk):
        return pltpu.make_async_copy(
            refs[part][0].at[0, pl.ds(chunk * size, size)], held.at[part, chunk], in_sem.at[part, chunk])

    def store(part, chunk):
        return pltpu.make_async_copy(
            held.at[part, chunk], refs[part][1].at[0, pl.ds(chunk * size, size)], out_sem.at[part, chunk])

    order = [(part, chunk) for chunk in range(chunks) for part in range(2)]
    for key in order:
        fetch(*key).start()
    for key in order:
        fetch(*key).wait()
        store(*key).start()
    for key in order:
        store(*key).wait()


def shards(counts, green_real, green_imag, coupling, strengths, offsets):
    energies, orbitals = green_real.shape[1], green_real.shape[2]
    hops, branches = coupling.shape[0], coupling.shape[1]
    pieces, _ = pieces_of(energies)
    anywhere = pl.BlockSpec(memory_space=pl.ANY)
    dma = pltpu.SemaphoreType.DMA
    chunks = len(pieces)
    square = (orbitals, orbitals)
    extended = (2, energies + 2 * REACH) + square
    shapes = [jax.ShapeDtypeStruct(green_real.shape, jnp.bfloat16)] * 2
    dressed = pl.pallas_call(
        functools.partial(kernel, counts),
        out_shape=shapes,
        in_specs=[anywhere] * 5,
        out_specs=[anywhere] * 2,
        scratch_shapes=[
            pltpu.VMEM((2, energies) + square, jnp.bfloat16),
            pltpu.VMEM(extended, jnp.bfloat16),
            pltpu.VMEM(extended, jnp.bfloat16),
            pltpu.VMEM(coupling.shape, jnp.bfloat16),
            pltpu.SMEM(strengths.shape, jnp.float32),
            pltpu.SMEM(offsets.shape, jnp.int32),
            pltpu.VMEM((hops, branches) + square, jnp.bfloat16),
            pltpu.VMEM((hops * branches,) + square, jnp.bfloat16),
            pltpu.VMEM((hops * branches * TAPS, LANES, orbitals), jnp.bfloat16),
            pltpu.VMEM((2, 2) + square, jnp.bfloat16),
            pltpu.VMEM((2 * REACH, hops * branches, 2) + square, jnp.bfloat16),
            pltpu.VMEM((REACH, hops * branches, 2) + square, jnp.bfloat16),
            pltpu.VMEM((2, energies) + square, jnp.bfloat16),
            dma((2,)), dma((3,)), dma((2,)),
            dma((2,)), dma((chunks, 2)),
            dma((2,)), dma((chunks,)),
            dma((hops, 2)), dma((hops, 2)),
            pltpu.SemaphoreType.REGULAR((2,)),
        ],
        compiler_params=pltpu.CompilerParams(
            collective_id=0, has_side_effects=True, vmem_limit_bytes=GRANT),
    )(green_real, green_imag, coupling, strengths, offsets)
    parts = 3 if energies % 3 == 0 else 1
    return pl.pallas_call(
        deliver,
        out_shape=shapes,
        in_specs=[anywhere] * 2,
        out_specs=[anywhere] * 2,
        scratch_shapes=[
            pltpu.VMEM((2, parts, energies // parts) + square, jnp.bfloat16),
            dma((2, parts)), dma((2, parts)),
        ],
        compiler_params=pltpu.CompilerParams(vmem_limit_bytes=GRANT),
    )(*dressed)


def solution(mesh):
    blocks = P("kz", "en", None, None)
    counts = (mesh.shape["kz"], mesh.shape["en"])
    return jax.shard_map(
        functools.partial(shards, counts), mesh=mesh,
        in_specs=(blocks, blocks, P(None, None, "kz", None, None), P(), P()),
        out_specs=(blocks, blocks), check_vma=False)
```

```python
import functools

import jax
import jax.numpy as jnp
from jax import lax
from jax.experimental import pallas as pl
from jax.experimental.pallas import tpu as pltpu
from jax.sharding import PartitionSpec as P

REACH = 4
TAPS = 2 * REACH + 1
TILE = 64
LANES = 16
SKEW = 2
MESH = pl.DeviceIdType.MESH
GRANT = 60 * 2**20


def pieces_of(energies):
    order = list(range(energies - REACH, energies)) + list(range(energies - REACH))
    pieces = [(energy, 1) for energy in order]
    edges = 2 * REACH
    return pieces, edges


def paired(real, imag):
    return jnp.concatenate(
        [jnp.concatenate([real, imag], axis=1), jnp.concatenate([-imag, real], axis=1)], axis=0)


def product_of(green_real, green_imag, real, imag):
    return jnp.dot(jnp.concatenate([green_real, green_imag], axis=1), paired(real, imag),
                   preferred_element_type=jnp.float32).astype(jnp.bfloat16)


def dressed_of(real, imag, prod):
    back = jnp.dot(prod, paired(real, imag), preferred_element_type=jnp.float32)
    orbitals = real.shape[-1]
    return ((real.astype(jnp.float32) + back[:, :orbitals]).astype(jnp.bfloat16),
            (imag.astype(jnp.float32) + back[:, orbitals:]).astype(jnp.bfloat16))


def kernel(counts, real_hbm, imag_hbm, coupling_hbm, strengths_hbm, offsets_hbm, real_out, imag_out, sigma_out,
           own, near, far, via, coupling, strengths, offsets, turned, flat, weights, sigma, partial, rotated, half, pending, final, dressed,
           own_sem, small_sem, out_sem, final_sem, far_send, far_recv, near_send, near_recv, halo_send, halo_recv, via_recv, forward_send, ack):
    momenta, sections = counts
    hops, branches, orbitals = coupling.shape[0], coupling.shape[1], coupling.shape[-1]
    energies = own.shape[1]
    last = energies - REACH - 1
    pieces, edges = pieces_of(energies)
    kz, en = lax.axis_index("kz"), lax.axis_index("en")
    odd = lax.rem(kz, 2)
    even = 1 - odd
    partner = kz + 1 - 2 * odd
    ahead, behind = lax.rem(kz + 2, momenta), lax.rem(kz + momenta - 2, momenta)
    has_low, has_high = en > 0, en < sections - 1
    sources, outs, fields = (real_hbm, imag_hbm), (real_out, imag_out), (near, far)

    barrier = pltpu.get_barrier_semaphore()
    pl.semaphore_signal(barrier, inc=1, device_id=(behind, en), device_id_type=MESH)

    @pl.when(even == 1)
    def _():
        pl.semaphore_signal(barrier, inc=1, device_id=(partner, en), device_id_type=MESH)

    @pl.when(has_high)
    def _():
        pl.semaphore_signal(barrier, inc=1, device_id=(kz, en + 1), device_id_type=MESH)

    smalls = [pltpu.make_async_copy(a, b, small_sem.at[i]) for i, (a, b) in enumerate(
        ((coupling_hbm, coupling), (strengths_hbm, strengths), (offsets_hbm, offsets)))]
    for copy in smalls:
        copy.start()
    pl.semaphore_wait(barrier, 1 + odd + has_low.astype(jnp.int32))

    def far_copy(piece, start, size, part):
        return pltpu.make_async_remote_copy(
            sources[part].at[0, pl.ds(start, size)], far.at[part, pl.ds(REACH + start, size)],
            far_send.at[part], far_recv.at[piece, part], device_id=(ahead, en), device_id_type=MESH)

    def near_copy(piece, start, size, part, relay):
        rows = pl.ds(REACH + start, size)
        source = far.at[part, rows] if relay else sources[part].at[0, pl.ds(start, size)]
        return pltpu.make_async_remote_copy(
            source, near.at[part, rows],
            near_send.at[part], near_recv.at[piece], device_id=(partner, en), device_id_type=MESH)

    def via_copy(part):
        return pltpu.make_async_remote_copy(
            sources[part].at[0, pl.ds(last, 1)], via.at[part], near_send.at[part], via_recv,
            device_id=(partner, en), device_id_type=MESH)

    def forward_copy():
        return pltpu.make_async_remote_copy(
            via, near.at[:, pl.ds(REACH + last, 1)], forward_send, near_recv.at[len(pieces) - 1],
            device_id=(ahead, en), device_id_type=MESH)

    def halo_copy(hop, side):
        field = fields[hop]
        if side == 0:
            source, target, to = energies, 0, lax.rem(en + 1, sections)
        else:
            source, target, to = REACH, REACH + energies, lax.rem(en + sections - 1, sections)
        return pltpu.make_async_remote_copy(
            field.at[:, pl.ds(source, REACH)], field.at[:, pl.ds(target, REACH)],
            halo_send.at[hop, side], halo_recv.at[hop, side], device_id=(kz, to), device_id_type=MESH)

    @pl.when(odd == 1)
    def _():
        pl.semaphore_signal(ack.at[0], inc=1, device_id=(partner, en), device_id_type=MESH)

    @pl.when(has_low)
    def _():
        pl.semaphore_signal(ack.at[1], inc=1, device_id=(kz, en - 1), device_id_type=MESH)

    def send_far(first, stop):
        for piece in range(first, stop):
            for part in range(2):
                far_copy(piece, *pieces[piece], part).start()

    def send_near(first, stop):
        @pl.when(odd == 0)
        def _():
            if first == 0:
                pl.semaphore_wait(ack.at[0], 1)
            for piece in range(first, stop):
                for part in range(2):
                    near_copy(piece, *pieces[piece], part, False).start()

    send_far(0, edges)

    @pl.when(odd == 1)
    def _():
        for part in range(2):
            via_copy(part).start()

    send_near(0, edges)
    send_far(edges, len(pieces))
    send_near(edges, len(pieces))

    owns = [pltpu.make_async_copy(sources[part].at[0], own.at[part], own_sem.at[part]) for part in range(2)]
    for copy in owns:
        copy.start()

    @pl.when(has_high)
    def _():
        pl.semaphore_wait(ack.at[1], 1)

    def arrive_far(piece, start, size, relay=True):
        for part in range(2):
            far_copy(piece, start, size, part).wait_recv()

            if relay:
                @pl.when(odd == 1)
                def _(part=part):
                    near_copy(piece, start, size, part, True).start()

    def arrive_near(piece, start, size):
        rows = pl.ds(REACH + start, size)
        pltpu.make_async_copy(near.at[:, rows], near.at[:, rows], near_recv.at[piece]).wait()

    def arrive(piece, start, size):
        arrive_far(piece, start, size)
        arrive_near(piece, start, size)

    zeros = jnp.zeros((2, REACH, orbitals, orbitals), jnp.bfloat16)
    blank = jnp.zeros((orbitals, orbitals), jnp.bfloat16)

    @pl.when(en == 0)
    def _():
        near[:, pl.ds(0, REACH)] = zeros
        far[:, pl.ds(0, REACH)] = zeros

    @pl.when(en == sections - 1)
    def _():
        near[:, pl.ds(REACH + energies, REACH)] = zeros
        far[:, pl.ds(REACH + energies, REACH)] = zeros

    def place_of(hop, branch):
        return hop * branches + branch

    def prepare(hop, branch):
        matrix = coupling[hop, branch, 0].astype(jnp.float32)
        turned[hop, branch] = matrix.T.astype(jnp.bfloat16)
        flat[place_of(hop, branch)] = (matrix * (1.0 / orbitals)).astype(jnp.bfloat16)
        for tap in range(TAPS):
            if tap == REACH:
                continue
            total = jnp.float32(0)
            for index in range(offsets.shape[1]):
                total = total + jnp.where(
                    offsets[hop, index] == REACH - tap, strengths[hop, branch, index], 0.0)
            weights[place_of(hop, branch) * TAPS + tap] = jnp.full(
                (LANES, orbitals), total, jnp.float32).astype(jnp.bfloat16)

    def scale_of(hop, branch, tap, rows):
        return jnp.concatenate([weights[place_of(hop, branch) * TAPS + tap]] * (rows // LANES), axis=0)

    every = [tap for tap in range(TAPS) if tap != REACH]

    def right(energy, hop, pair, taps):
        field = fields[hop]
        both = (2 * pair, 2 * pair + 1)
        rows = []
        for part in range(2):
            for row in range(0, orbitals, TILE):
                sums = [None, None]
                for first in range(0, len(taps), 2):
                    some = taps[first:first + 2]
                    windows = [field[part, energy + tap, row:row + TILE, :] for tap in some]
                    for index, branch in enumerate(both):
                        terms = [scale_of(hop, branch, tap, TILE) * window for tap, window in zip(some, windows)]
                        term = terms[0] if len(terms) == 1 else terms[0] + terms[1]
                        sums[index] = term if sums[index] is None else sums[index] + term
                rows.append(jnp.concatenate(sums, axis=1))
        blocks = jnp.concatenate([jnp.concatenate([turned[hop, both[0]], blank], axis=1),
                                  jnp.concatenate([blank, turned[hop, both[1]]], axis=1)], axis=0)
        made = jnp.dot(jnp.concatenate(rows, axis=0), blocks, preferred_element_type=jnp.float32).astype(jnp.bfloat16)
        return [jnp.concatenate([made[:orbitals, side:side + orbitals], made[orbitals:, side:side + orbitals]], axis=1)
                for side in (0, orbitals)]

    def left(parts, hop=None):
        places = range(hops * branches) if hop is None else range(hop * branches, (hop + 1) * branches)
        return jnp.dot(jnp.concatenate([flat[place] for place in places], axis=1),
                       jnp.concatenate(parts, axis=0), preferred_element_type=jnp.float32)

    def rounded(total):
        total = total.astype(jnp.bfloat16)
        return total[:, :orbitals], total[:, orbitals:]

    def product(energy, real, imag):
        return product_of(own[0, energy], own[1, energy], real, imag)

    def dress(energy, prod):
        dressed[0, energy], dressed[1, energy] = dressed_of(own[0, energy], own[1, energy], prod)

    def part_of(energy, hop):
        parts = []
        for pair in range(branches // 2):
            parts += right(energy, hop, pair, every)
        return left(parts, hop)

    def stage(energy, slot, before, following):
        if before is not None:
            prod = product(before, sigma[1 - slot, 0], sigma[1 - slot, 1])
        sigma[slot, 0], sigma[slot, 1] = rounded(pending[slot] + part_of(energy, 0))
        if before is not None:
            dress(before, prod)
        if following is not None:
            pending[slot] = sum(part_of(following, hop) for hop in range(1, hops))

    tail = range(last - REACH, energies)

    def begin(energy, until, hop):
        taps = [tap for tap in every if not until < energy + tap - REACH <= last]
        for pair in range(branches // 2):
            for branch, value in zip((2 * pair, 2 * pair + 1), right(energy, hop, pair, taps)):
                for part in range(2):
                    partial[tail.index(energy), place_of(hop, branch), part] = (
                        value[:, part * orbitals:(part + 1) * orbitals])

    def ready(energy):
        return last - REACH if energy >= last else energy - 1

    def rotate(source, hop):
        rows = jnp.concatenate([fields[hop][0, REACH + source], fields[hop][1, REACH + source]], axis=0)
        for pair in range(branches // 2):
            first, second = 2 * pair, 2 * pair + 1
            both = jnp.dot(rows, jnp.concatenate([turned[hop, first], turned[hop, second]], axis=1),
                           preferred_element_type=jnp.float32).astype(jnp.bfloat16)
            for index, branch in enumerate((first, second)):
                for part in range(2):
                    rotated[last - source, place_of(hop, branch), part] = both[
                        part * orbitals:(part + 1) * orbitals, index * orbitals:(index + 1) * orbitals]

    def updated(energy, hop, branch, part):
        place = place_of(hop, branch)
        total = None
        for source in range(last - REACH + 1, last + 1):
            if source > ready(energy) and source != energy and abs(source - energy) <= REACH:
                term = scale_of(hop, branch, source - energy + REACH, orbitals) * rotated[last - source, place, part]
                total = term if total is None else total + term
        return total + partial[tail.index(energy), place, part]

    def out_copy(start, size, part):
        return pltpu.make_async_copy(
            dressed.at[part, pl.ds(start, size)], outs[part].at[0, pl.ds(start, size)], out_sem.at[part])

    def out(start, size):
        for part in range(2):
            out_copy(start, size, part).start()

    def halo_out(hop, side, cond):
        @pl.when(cond)
        def _():
            halo_copy(hop, side).start()

    def halo_in(side, cond):
        @pl.when(cond)
        def _():
            for hop in range(hops):
                halo_copy(hop, side).wait_recv()

    jobs = [(hop, branch) for hop in range(hops) for branch in range(branches)]
    for piece in range(edges):
        arrive(piece, *pieces[piece])
        if piece == 1:
            @pl.when(odd == 0)
            def _():
                pltpu.make_async_copy(via, via, via_recv).wait()
                forward_copy().start()
        if piece == REACH - 1:
            for hop in range(hops):
                halo_out(hop, 0, has_high)
        if piece == edges - 1:
            for hop in range(hops):
                halo_out(hop, 1, has_low)
        if piece == 0:
            for copy in smalls:
                copy.wait()
        for job in jobs[piece::edges]:
            prepare(*job)
    for copy in owns:
        copy.wait()

    piece, start = edges, REACH
    stages = 0

    def step(energy):
        stage(energy, energy % 2, energy - 1 if energy > 0 else None, energy + SKEW if energy + SKEW < tail[0] else None)

    halo_in(0, has_low)
    count = last - 1 - 2 * REACH
    for energy in range(SKEW):
        arrive_far(piece + energy, start + energy, 1)
        pending[energy % 2] = sum(part_of(energy, hop) for hop in range(1, hops))
    for energy in range(2 - count % 2):
        arrive_far(piece + SKEW, start + SKEW, 1)
        arrive_near(piece, start, 1)
        step(energy)
        stages, start, piece = stages + 1, start + 1, piece + 1
    pairs = (count - stages) // 2
    if stages > 1:
        out(0, stages - 1)

    base_piece, base_start, parity = piece, start, stages % 2

    def body(index, carry):
        first = base_start + 2 * index
        for offset in range(2):
            arrive_far(base_piece + 2 * index + offset + SKEW, first + offset + SKEW, 1)
            arrive_near(base_piece + 2 * index + offset, first + offset, 1)
            energy = first - REACH + offset
            stage(energy, (parity + offset) % 2, energy - 1, energy + SKEW)
        for part in range(2):
            out_copy(first - REACH - 1, 2, part).start()
        return carry

    split = pairs - 1
    lax.fori_loop(0, split, body, 0)
    halo_in(1, has_high)
    upper = list(range(last + 1, energies))
    for energy in upper[:2]:
        for hop in range(hops):
            begin(energy, last - REACH, hop)
    lax.fori_loop(split, pairs, body, 0)
    for energy in upper[2:]:
        for hop in range(hops):
            begin(energy, last - REACH, hop)
    piece, start, stages = piece + 2 * pairs, start + 2 * pairs, stages + 2 * pairs

    def opened(source, hop):
        if last - REACH <= source + 1 < last:
            begin(source + 1, source, hop)
        if source == last - REACH:
            begin(last, source, hop)
        if source > last - REACH:
            rotate(source, hop)

    def late(energy, hop):
        return left([jnp.concatenate([updated(energy, hop, branch, part) for part in range(2)], axis=1)
                     for branch in range(branches)], hop)

    def halves():
        for index, energy in enumerate(tail):
            half[index] = sum(late(energy, hop) for hop in range(1, hops))

    for source in range(start, start + SKEW):
        for hop in range(1, hops):
            opened(source, hop)
    for source in range(start, last):
        if source + SKEW <= last:
            arrive_far(piece + SKEW, source + SKEW, 1, source + SKEW < last)
        else:
            halves()
        arrive_near(piece, source, 1)
        step(stages)
        opened(source, 0)
        if source + SKEW <= last:
            for hop in range(1, hops):
                opened(source + SKEW, hop)
        out(stages - 1, 1)
        stages += 1
        piece += 1
    for side, cond in ((0, has_high), (1, has_low)):
        @pl.when(cond)
        def _(side=side):
            for hop in range(hops):
                halo_copy(hop, side).wait_send()
    before = stages - 1
    dress(before, product(before, sigma[before % 2, 0], sigma[before % 2, 1]))
    out(before, 1)
    arrive_near(piece, last, 1)
    rotate(last, 0)

    def final_copy(first, size):
        rows = pl.ds(first, size)
        return pltpu.make_async_copy(final.at[rows], sigma_out.at[rows], final_sem)

    for index, energy in enumerate(tail):
        final[index, 0], final[index, 1] = rounded(half[index] + late(energy, 0))
        final_copy(index, 1).start()

    for part in range(2):
        far_copy(0, 0, energies, part).wait_send()
        near_copy(0, 0, energies, part, False).wait_send()
        out_copy(0, stages, part).wait()
    final_copy(0, len(tail)).wait()

    @pl.when(odd == 0)
    def _():
        forward_copy().wait_send()


def deliver(real_in, imag_in, sigma_in, real_hbm, imag_hbm, real_out, imag_out,
            held, own, sigma, dressed, own_sem, sigma_sem, in_sem, out_sem):
    count, early = sigma.shape[0], held.shape[1]
    ins, greens, outs = (real_in, imag_in), (real_hbm, imag_hbm), (real_out, imag_out)
    blocks = [(0, count // 3), (count // 3, count - count // 3)]

    def own_copy(part, block):
        return pltpu.make_async_copy(greens[part].at[0, pl.ds(early + blocks[block][0], blocks[block][1])],
                                     own.at[part, pl.ds(*blocks[block])], own_sem.at[block, part])

    def sigma_copy(block):
        return pltpu.make_async_copy(sigma_in.at[pl.ds(*blocks[block])], sigma.at[pl.ds(*blocks[block])], sigma_sem.at[block])

    fetches = [pltpu.make_async_copy(ins[part].at[0], held.at[part], in_sem.at[part]) for part in range(2)]
    arrivals = [[sigma_copy(block), own_copy(0, block), own_copy(1, block)] for block in range(2)]
    for copy in (*arrivals[0], *arrivals[1], *fetches):
        copy.start()
    for block, (first, size) in enumerate(blocks):
        for copy in arrivals[block]:
            copy.wait()
        if block == 1:
            for part in range(2):
                fetches[part].wait()
                pltpu.make_async_copy(held.at[part], outs[part].at[0, pl.ds(0, early)], out_sem.at[part]).start()
        prods = [product_of(own[0, index], own[1, index], sigma[index, 0], sigma[index, 1])
                 for index in range(first, first + size)]
        for index, prod in enumerate(prods, first):
            dressed[0, index], dressed[1, index] = dressed_of(own[0, index], own[1, index], prod)
        for part in range(2):
            pltpu.make_async_copy(dressed.at[part, pl.ds(first, size)],
                                  outs[part].at[0, pl.ds(early + first, size)], out_sem.at[part]).start()
    for part in range(2):
        pltpu.make_async_copy(outs[part].at[0], outs[part].at[0], out_sem.at[part]).wait()


def shards(counts, green_real, green_imag, coupling, strengths, offsets):
    energies, orbitals = green_real.shape[1], green_real.shape[2]
    hops, branches = coupling.shape[0], coupling.shape[1]
    pieces, _ = pieces_of(energies)
    anywhere = pl.BlockSpec(memory_space=pl.ANY)
    dma = pltpu.SemaphoreType.DMA
    chunks = len(pieces)
    square = (orbitals, orbitals)
    extended = (2, energies + 2 * REACH) + square
    count = 2 * REACH + 1
    early = energies - count
    shapes = [jax.ShapeDtypeStruct(green_real.shape, jnp.bfloat16)] * 2
    made = pl.pallas_call(
        functools.partial(kernel, counts),
        out_shape=[jax.ShapeDtypeStruct((1, early) + square, jnp.bfloat16)] * 2
        + [jax.ShapeDtypeStruct((count, 2) + square, jnp.bfloat16)],
        in_specs=[anywhere] * 5,
        out_specs=[anywhere] * 3,
        scratch_shapes=[
            pltpu.VMEM((2, energies) + square, jnp.bfloat16),
            pltpu.VMEM(extended, jnp.bfloat16),
            pltpu.VMEM(extended, jnp.bfloat16),
            pltpu.VMEM((2, 1) + square, jnp.bfloat16),
            pltpu.VMEM(coupling.shape, jnp.bfloat16),
            pltpu.SMEM(strengths.shape, jnp.float32),
            pltpu.SMEM(offsets.shape, jnp.int32),
            pltpu.VMEM((hops, branches) + square, jnp.bfloat16),
            pltpu.VMEM((hops * branches,) + square, jnp.bfloat16),
            pltpu.VMEM((hops * branches * TAPS, LANES, orbitals), jnp.bfloat16),
            pltpu.VMEM((2, 2) + square, jnp.bfloat16),
            pltpu.VMEM((2 * REACH + 1, hops * branches, 2) + square, jnp.bfloat16),
            pltpu.VMEM((REACH, hops * branches, 2) + square, jnp.bfloat16),
            pltpu.VMEM((2 * REACH + 1, orbitals, 2 * orbitals), jnp.float32),
            pltpu.VMEM((2, orbitals, 2 * orbitals), jnp.float32),
            pltpu.VMEM((count, 2) + square, jnp.bfloat16),
            pltpu.VMEM((2, early) + square, jnp.bfloat16),
            dma((2,)), dma((3,)), dma((2,)), dma,
            dma((2,)), dma((chunks, 2)),
            dma((2,)), dma((chunks,)),
            dma((hops, 2)), dma((hops, 2)), dma, dma,
            pltpu.SemaphoreType.REGULAR((2,)),
        ],
        compiler_params=pltpu.CompilerParams(
            collective_id=0, has_side_effects=True, vmem_limit_bytes=GRANT),
    )(green_real, green_imag, coupling, strengths, offsets)
    return pl.pallas_call(
        deliver,
        out_shape=shapes,
        in_specs=[anywhere] * 5,
        out_specs=[anywhere] * 2,
        scratch_shapes=[
            pltpu.VMEM((2, early) + square, jnp.bfloat16),
            pltpu.VMEM((2, count) + square, jnp.bfloat16),
            pltpu.VMEM((count, 2) + square, jnp.bfloat16),
            pltpu.VMEM((2, count) + square, jnp.bfloat16),
            dma((2, 2)), dma((2,)), dma((2,)), dma((2,)),
        ],
        compiler_params=pltpu.CompilerParams(vmem_limit_bytes=GRANT),
    )(*made, green_real, green_imag)


def solution(mesh):
    blocks = P("kz", "en", None, None)
    counts = (mesh.shape["kz"], mesh.shape["en"])
    return jax.shard_map(
        functools.partial(shards, counts), mesh=mesh,
        in_specs=(blocks, blocks, P(None, None, "kz", None, None), P(), P()),
        out_specs=(blocks, blocks), check_vma=False)
```

```python
import functools

import jax
import jax.numpy as jnp
from jax import lax
from jax.experimental import pallas as pl
from jax.experimental.pallas import tpu as pltpu
from jax.sharding import PartitionSpec as P

REACH = 4
TAPS = 2 * REACH + 1
TILE = 64
LANES = 16
SKEW = 2
MESH = pl.DeviceIdType.MESH
GRANT = 60 * 2**20


def pieces_of(energies):
    order = list(range(energies - REACH, energies)) + list(range(energies - REACH))
    pieces = [(energy, 1) for energy in order]
    edges = 2 * REACH
    return pieces, edges


def paired(real, imag):
    return jnp.concatenate(
        [jnp.concatenate([real, imag], axis=1), jnp.concatenate([-imag, real], axis=1)], axis=0)


def product_of(green_real, green_imag, real, imag):
    return jnp.dot(jnp.concatenate([green_real, green_imag], axis=1), paired(real, imag),
                   preferred_element_type=jnp.float32).astype(jnp.bfloat16)


def dressed_of(real, imag, prod):
    back = jnp.dot(prod, paired(real, imag), preferred_element_type=jnp.float32)
    orbitals = real.shape[-1]
    return ((real.astype(jnp.float32) + back[:, :orbitals]).astype(jnp.bfloat16),
            (imag.astype(jnp.float32) + back[:, orbitals:]).astype(jnp.bfloat16))


def kernel(counts, real_hbm, imag_hbm, coupling_hbm, strengths_hbm, offsets_hbm, real_out, imag_out, sigma_out,
           own, near, far, via, coupling, strengths, offsets, turned, flat, weights, sigma, partial, rotated, half, pending, final, dressed,
           own_sem, small_sem, out_sem, final_sem, far_send, far_recv, near_send, near_recv, halo_send, halo_recv, via_recv, forward_send, ack):
    momenta, sections = counts
    hops, branches, orbitals = coupling.shape[0], coupling.shape[1], coupling.shape[-1]
    energies = own.shape[1]
    last = energies - REACH - 1
    pieces, edges = pieces_of(energies)
    kz, en = lax.axis_index("kz"), lax.axis_index("en")
    odd = lax.rem(kz, 2)
    even = 1 - odd
    partner = kz + 1 - 2 * odd
    ahead, behind = lax.rem(kz + 2, momenta), lax.rem(kz + momenta - 2, momenta)
    has_low, has_high = en > 0, en < sections - 1
    sources, outs, fields = (real_hbm, imag_hbm), (real_out, imag_out), (near, far)

    barrier = pltpu.get_barrier_semaphore()
    pl.semaphore_signal(barrier, inc=1, device_id=(behind, en), device_id_type=MESH)

    @pl.when(even == 1)
    def _():
        pl.semaphore_signal(barrier, inc=1, device_id=(partner, en), device_id_type=MESH)

    @pl.when(has_high)
    def _():
        pl.semaphore_signal(barrier, inc=1, device_id=(kz, en + 1), device_id_type=MESH)

    smalls = [pltpu.make_async_copy(a, b, small_sem.at[i]) for i, (a, b) in enumerate(
        ((coupling_hbm, coupling), (strengths_hbm, strengths), (offsets_hbm, offsets)))]
    pl.semaphore_wait(barrier, 1 + odd + has_low.astype(jnp.int32))

    def far_copy(piece, start, size, part):
        return pltpu.make_async_remote_copy(
            sources[part].at[0, pl.ds(start, size)], far.at[part, pl.ds(REACH + start, size)],
            far_send.at[part], far_recv.at[piece, part], device_id=(ahead, en), device_id_type=MESH)

    def near_copy(piece, start, size, part, relay):
        rows = pl.ds(REACH + start, size)
        source = far.at[part, rows] if relay else sources[part].at[0, pl.ds(start, size)]
        return pltpu.make_async_remote_copy(
            source, near.at[part, rows],
            near_send.at[part], near_recv.at[piece], device_id=(partner, en), device_id_type=MESH)

    def via_copy(part):
        return pltpu.make_async_remote_copy(
            sources[part].at[0, pl.ds(last, 1)], via.at[part], near_send.at[part], via_recv,
            device_id=(partner, en), device_id_type=MESH)

    def forward_copy():
        return pltpu.make_async_remote_copy(
            via, near.at[:, pl.ds(REACH + last, 1)], forward_send, near_recv.at[len(pieces) - 1],
            device_id=(ahead, en), device_id_type=MESH)

    def halo_copy(hop, side):
        field = fields[hop]
        if side == 0:
            source, target, to = energies, 0, lax.rem(en + 1, sections)
        else:
            source, target, to = REACH, REACH + energies, lax.rem(en + sections - 1, sections)
        return pltpu.make_async_remote_copy(
            field.at[:, pl.ds(source, REACH)], field.at[:, pl.ds(target, REACH)],
            halo_send.at[hop, side], halo_recv.at[hop, side], device_id=(kz, to), device_id_type=MESH)

    @pl.when(odd == 1)
    def _():
        pl.semaphore_signal(ack.at[0], inc=1, device_id=(partner, en), device_id_type=MESH)

    @pl.when(has_low)
    def _():
        pl.semaphore_signal(ack.at[1], inc=1, device_id=(kz, en - 1), device_id_type=MESH)

    def send_far(first, stop):
        for piece in range(first, stop):
            for part in range(2):
                far_copy(piece, *pieces[piece], part).start()

    def send_near(first, stop):
        @pl.when(odd == 0)
        def _():
            if first == 0:
                pl.semaphore_wait(ack.at[0], 1)
            for piece in range(first, stop):
                for part in range(2):
                    near_copy(piece, *pieces[piece], part, False).start()

    send_far(0, edges)

    @pl.when(odd == 1)
    def _():
        for part in range(2):
            via_copy(part).start()

    send_near(0, edges)
    for copy in smalls:
        copy.start()
    send_far(edges, len(pieces))
    send_near(edges, len(pieces))

    owns = [pltpu.make_async_copy(sources[part].at[0], own.at[part], own_sem.at[part]) for part in range(2)]
    for copy in owns:
        copy.start()

    @pl.when(has_high)
    def _():
        pl.semaphore_wait(ack.at[1], 1)

    def arrive_far(piece, start, size, relay=True):
        for part in range(2):
            far_copy(piece, start, size, part).wait_recv()

            if relay:
                @pl.when(odd == 1)
                def _(part=part):
                    near_copy(piece, start, size, part, True).start()

    def arrive_near(piece, start, size):
        rows = pl.ds(REACH + start, size)
        pltpu.make_async_copy(near.at[:, rows], near.at[:, rows], near_recv.at[piece]).wait()

    def arrive(piece, start, size):
        arrive_far(piece, start, size)
        arrive_near(piece, start, size)

    zeros = jnp.zeros((2, REACH, orbitals, orbitals), jnp.bfloat16)
    blank = jnp.zeros((orbitals, orbitals), jnp.bfloat16)

    @pl.when(en == 0)
    def _():
        near[:, pl.ds(0, REACH)] = zeros
        far[:, pl.ds(0, REACH)] = zeros

    @pl.when(en == sections - 1)
    def _():
        near[:, pl.ds(REACH + energies, REACH)] = zeros
        far[:, pl.ds(REACH + energies, REACH)] = zeros

    def place_of(hop, branch):
        return hop * branches + branch

    def prepare(hop, branch):
        matrix = coupling[hop, branch, 0].astype(jnp.float32)
        turned[hop, branch] = matrix.T.astype(jnp.bfloat16)
        flat[place_of(hop, branch)] = (matrix * (1.0 / orbitals)).astype(jnp.bfloat16)
        for tap in range(TAPS):
            if tap == REACH:
                continue
            total = jnp.float32(0)
            for index in range(offsets.shape[1]):
                total = total + jnp.where(
                    offsets[hop, index] == REACH - tap, strengths[hop, branch, index], 0.0)
            weights[place_of(hop, branch) * TAPS + tap] = jnp.full(
                (LANES, orbitals), total, jnp.float32).astype(jnp.bfloat16)

    def scale_of(hop, branch, tap, rows):
        return jnp.concatenate([weights[place_of(hop, branch) * TAPS + tap]] * (rows // LANES), axis=0)

    every = [tap for tap in range(TAPS) if tap != REACH]

    def right(energy, hop, pair, taps):
        field = fields[hop]
        both = (2 * pair, 2 * pair + 1)
        rows = []
        for part in range(2):
            for row in range(0, orbitals, TILE):
                sums = [None, None]
                for first in range(0, len(taps), 2):
                    some = taps[first:first + 2]
                    windows = [field[part, energy + tap, row:row + TILE, :] for tap in some]
                    for index, branch in enumerate(both):
                        terms = [scale_of(hop, branch, tap, TILE) * window for tap, window in zip(some, windows)]
                        term = terms[0] if len(terms) == 1 else terms[0] + terms[1]
                        sums[index] = term if sums[index] is None else sums[index] + term
                rows.append(jnp.concatenate(sums, axis=1))
        blocks = jnp.concatenate([jnp.concatenate([turned[hop, both[0]], blank], axis=1),
                                  jnp.concatenate([blank, turned[hop, both[1]]], axis=1)], axis=0)
        made = jnp.dot(jnp.concatenate(rows, axis=0), blocks, preferred_element_type=jnp.float32).astype(jnp.bfloat16)
        return [jnp.concatenate([made[:orbitals, side:side + orbitals], made[orbitals:, side:side + orbitals]], axis=1)
                for side in (0, orbitals)]

    def left(parts, hop=None):
        places = range(hops * branches) if hop is None else range(hop * branches, (hop + 1) * branches)
        return jnp.dot(jnp.concatenate([flat[place] for place in places], axis=1),
                       jnp.concatenate(parts, axis=0), preferred_element_type=jnp.float32)

    def rounded(total):
        total = total.astype(jnp.bfloat16)
        return total[:, :orbitals], total[:, orbitals:]

    def product(energy, real, imag):
        return product_of(own[0, energy], own[1, energy], real, imag)

    def dress(energy, prod):
        dressed[0, energy], dressed[1, energy] = dressed_of(own[0, energy], own[1, energy], prod)

    def part_of(energy, hop):
        parts = []
        for pair in range(branches // 2):
            parts += right(energy, hop, pair, every)
        return left(parts, hop)

    def stage(energy, slot, before, following):
        if before is not None:
            prod = product(before, sigma[1 - slot, 0], sigma[1 - slot, 1])
        sigma[slot, 0], sigma[slot, 1] = rounded(pending[slot] + part_of(energy, 0))
        if before is not None:
            dress(before, prod)
        if following is not None:
            pending[slot] = sum(part_of(following, hop) for hop in range(1, hops))

    tail = range(last - REACH, energies)

    def begin(energy, until, hop):
        taps = [tap for tap in every if not until < energy + tap - REACH <= last]
        for pair in range(branches // 2):
            for branch, value in zip((2 * pair, 2 * pair + 1), right(energy, hop, pair, taps)):
                for part in range(2):
                    partial[tail.index(energy), place_of(hop, branch), part] = (
                        value[:, part * orbitals:(part + 1) * orbitals])

    def ready(energy):
        return last - REACH if energy >= last else energy - 1

    def rotate(source, hop):
        rows = jnp.concatenate([fields[hop][0, REACH + source], fields[hop][1, REACH + source]], axis=0)
        for pair in range(branches // 2):
            first, second = 2 * pair, 2 * pair + 1
            both = jnp.dot(rows, jnp.concatenate([turned[hop, first], turned[hop, second]], axis=1),
                           preferred_element_type=jnp.float32).astype(jnp.bfloat16)
            for index, branch in enumerate((first, second)):
                for part in range(2):
                    rotated[last - source, place_of(hop, branch), part] = both[
                        part * orbitals:(part + 1) * orbitals, index * orbitals:(index + 1) * orbitals]

    def updated(energy, hop, branch, part):
        place = place_of(hop, branch)
        total = None
        for source in range(last - REACH + 1, last + 1):
            if source > ready(energy) and source != energy and abs(source - energy) <= REACH:
                term = scale_of(hop, branch, source - energy + REACH, orbitals) * rotated[last - source, place, part]
                total = term if total is None else total + term
        return total + partial[tail.index(energy), place, part]

    def out_copy(start, size, part):
        return pltpu.make_async_copy(
            dressed.at[part, pl.ds(start, size)], outs[part].at[0, pl.ds(start, size)], out_sem.at[part])

    def out(start, size):
        for part in range(2):
            out_copy(start, size, part).start()

    def halo_out(hop, side, cond):
        @pl.when(cond)
        def _():
            halo_copy(hop, side).start()

    def halo_in(side, cond):
        @pl.when(cond)
        def _():
            for hop in range(hops):
                halo_copy(hop, side).wait_recv()

    jobs = [(hop, branch) for hop in range(hops) for branch in range(branches)]
    for piece in range(edges):
        arrive(piece, *pieces[piece])
        if piece == 1:
            @pl.when(odd == 0)
            def _():
                pltpu.make_async_copy(via, via, via_recv).wait()
                forward_copy().start()
        if piece == REACH - 1:
            for hop in range(hops):
                halo_out(hop, 0, has_high)
        if piece == edges - 1:
            for hop in range(hops):
                halo_out(hop, 1, has_low)
        if piece == 0:
            for copy in smalls:
                copy.wait()
        for job in jobs[piece::edges]:
            prepare(*job)
    for copy in owns:
        copy.wait()

    piece, start = edges, REACH
    stages = 0

    def step(energy):
        stage(energy, energy % 2, energy - 1 if energy > 0 else None, energy + SKEW if energy + SKEW < tail[0] else None)

    halo_in(0, has_low)
    count = last - 1 - 2 * REACH
    for energy in range(SKEW):
        arrive_far(piece + energy, start + energy, 1)
        pending[energy % 2] = sum(part_of(energy, hop) for hop in range(1, hops))
    for energy in range(2 - count % 2):
        arrive_far(piece + SKEW, start + SKEW, 1)
        arrive_near(piece, start, 1)
        step(energy)
        stages, start, piece = stages + 1, start + 1, piece + 1
    pairs = (count - stages) // 2
    if stages > 1:
        out(0, stages - 1)

    base_piece, base_start, parity = piece, start, stages % 2

    def body(index, carry):
        first = base_start + 2 * index
        for offset in range(2):
            arrive_far(base_piece + 2 * index + offset + SKEW, first + offset + SKEW, 1)
            arrive_near(base_piece + 2 * index + offset, first + offset, 1)
            energy = first - REACH + offset
            stage(energy, (parity + offset) % 2, energy - 1, energy + SKEW)
        for part in range(2):
            out_copy(first - REACH - 1, 2, part).start()
        return carry

    split = pairs - 1
    lax.fori_loop(0, split, body, 0)
    halo_in(1, has_high)
    upper = list(range(last + 1, energies))
    for energy in upper[:2]:
        for hop in range(hops):
            begin(energy, last - REACH, hop)
    lax.fori_loop(split, pairs, body, 0)
    for energy in upper[2:]:
        for hop in range(hops):
            begin(energy, last - REACH, hop)
    piece, start, stages = piece + 2 * pairs, start + 2 * pairs, stages + 2 * pairs

    def opened(source, hop):
        if last - REACH <= source + 1 < last:
            begin(source + 1, source, hop)
        if source == last - REACH:
            begin(last, source, hop)
        if source > last - REACH:
            rotate(source, hop)

    def late(energy, hop):
        return left([jnp.concatenate([updated(energy, hop, branch, part) for part in range(2)], axis=1)
                     for branch in range(branches)], hop)

    def halves():
        for index, energy in enumerate(tail):
            half[index] = sum(late(energy, hop) for hop in range(1, hops))

    for source in range(start, start + SKEW):
        for hop in range(1, hops):
            opened(source, hop)
    for source in range(start, last):
        if source + SKEW <= last:
            arrive_far(piece + SKEW, source + SKEW, 1, source + SKEW < last)
        elif source == last - 1:
            halves()
            arrive_near(piece + 1, last, 1)
            rotate(last, 0)
        arrive_near(piece, source, 1)
        step(stages)
        opened(source, 0)
        if source + SKEW <= last:
            for hop in range(1, hops):
                opened(source + SKEW, hop)
        out(stages - 1, 1)
        stages += 1
        piece += 1
    for side, cond in ((0, has_high), (1, has_low)):
        @pl.when(cond)
        def _(side=side):
            for hop in range(hops):
                halo_copy(hop, side).wait_send()
    before = stages - 1
    dress(before, product(before, sigma[before % 2, 0], sigma[before % 2, 1]))
    out(before, 1)

    def final_copy(first, size):
        rows = pl.ds(first, size)
        return pltpu.make_async_copy(final.at[rows], sigma_out.at[rows], final_sem)

    for index, energy in enumerate(tail):
        final[index, 0], final[index, 1] = rounded(half[index] + late(energy, 0))
        final_copy(index, 1).start()

    for part in range(2):
        far_copy(0, 0, energies, part).wait_send()
        near_copy(0, 0, energies, part, False).wait_send()
        out_copy(0, stages, part).wait()
    final_copy(0, len(tail)).wait()

    @pl.when(odd == 0)
    def _():
        forward_copy().wait_send()


def deliver(real_in, imag_in, sigma_in, real_hbm, imag_hbm, real_out, imag_out,
            held, own, sigma, dressed, own_sem, sigma_sem, in_sem, out_sem):
    count, early = sigma.shape[0], held.shape[1]
    ins, greens, outs = (real_in, imag_in), (real_hbm, imag_hbm), (real_out, imag_out)
    blocks = [(0, count // 3), (count // 3, count - count // 3)]

    def own_copy(part, block):
        return pltpu.make_async_copy(greens[part].at[0, pl.ds(early + blocks[block][0], blocks[block][1])],
                                     own.at[part, pl.ds(*blocks[block])], own_sem.at[block, part])

    def sigma_copy(block):
        return pltpu.make_async_copy(sigma_in.at[pl.ds(*blocks[block])], sigma.at[pl.ds(*blocks[block])], sigma_sem.at[block])

    fetches = [pltpu.make_async_copy(ins[part].at[0], held.at[part], in_sem.at[part]) for part in range(2)]
    arrivals = [[sigma_copy(block), own_copy(0, block), own_copy(1, block)] for block in range(2)]
    for copy in (*arrivals[0], *arrivals[1], *fetches):
        copy.start()
    for block, (first, size) in enumerate(blocks):
        for copy in arrivals[block]:
            copy.wait()
        if block == 1:
            for part in range(2):
                fetches[part].wait()
                pltpu.make_async_copy(held.at[part], outs[part].at[0, pl.ds(0, early)], out_sem.at[part]).start()
        prods = [product_of(own[0, index], own[1, index], sigma[index, 0], sigma[index, 1])
                 for index in range(first, first + size)]
        for index, prod in enumerate(prods, first):
            dressed[0, index], dressed[1, index] = dressed_of(own[0, index], own[1, index], prod)
        for part in range(2):
            pltpu.make_async_copy(dressed.at[part, pl.ds(first, size)],
                                  outs[part].at[0, pl.ds(early + first, size)], out_sem.at[part]).start()
    for part in range(2):
        pltpu.make_async_copy(outs[part].at[0], outs[part].at[0], out_sem.at[part]).wait()


def shards(counts, green_real, green_imag, coupling, strengths, offsets):
    energies, orbitals = green_real.shape[1], green_real.shape[2]
    hops, branches = coupling.shape[0], coupling.shape[1]
    pieces, _ = pieces_of(energies)
    anywhere = pl.BlockSpec(memory_space=pl.ANY)
    dma = pltpu.SemaphoreType.DMA
    chunks = len(pieces)
    square = (orbitals, orbitals)
    extended = (2, energies + 2 * REACH) + square
    count = 2 * REACH + 1
    early = energies - count
    shapes = [jax.ShapeDtypeStruct(green_real.shape, jnp.bfloat16)] * 2
    made = pl.pallas_call(
        functools.partial(kernel, counts),
        out_shape=[jax.ShapeDtypeStruct((1, early) + square, jnp.bfloat16)] * 2
        + [jax.ShapeDtypeStruct((count, 2) + square, jnp.bfloat16)],
        in_specs=[anywhere] * 5,
        out_specs=[anywhere] * 3,
        scratch_shapes=[
            pltpu.VMEM((2, energies) + square, jnp.bfloat16),
            pltpu.VMEM(extended, jnp.bfloat16),
            pltpu.VMEM(extended, jnp.bfloat16),
            pltpu.VMEM((2, 1) + square, jnp.bfloat16),
            pltpu.VMEM(coupling.shape, jnp.bfloat16),
            pltpu.SMEM(strengths.shape, jnp.float32),
            pltpu.SMEM(offsets.shape, jnp.int32),
            pltpu.VMEM((hops, branches) + square, jnp.bfloat16),
            pltpu.VMEM((hops * branches,) + square, jnp.bfloat16),
            pltpu.VMEM((hops * branches * TAPS, LANES, orbitals), jnp.bfloat16),
            pltpu.VMEM((2, 2) + square, jnp.bfloat16),
            pltpu.VMEM((2 * REACH + 1, hops * branches, 2) + square, jnp.bfloat16),
            pltpu.VMEM((REACH, hops * branches, 2) + square, jnp.bfloat16),
            pltpu.VMEM((2 * REACH + 1, orbitals, 2 * orbitals), jnp.float32),
            pltpu.VMEM((2, orbitals, 2 * orbitals), jnp.float32),
            pltpu.VMEM((count, 2) + square, jnp.bfloat16),
            pltpu.VMEM((2, early) + square, jnp.bfloat16),
            dma((2,)), dma((3,)), dma((2,)), dma,
            dma((2,)), dma((chunks, 2)),
            dma((2,)), dma((chunks,)),
            dma((hops, 2)), dma((hops, 2)), dma, dma,
            pltpu.SemaphoreType.REGULAR((2,)),
        ],
        compiler_params=pltpu.CompilerParams(
            collective_id=0, has_side_effects=True, vmem_limit_bytes=GRANT),
    )(green_real, green_imag, coupling, strengths, offsets)
    return pl.pallas_call(
        deliver,
        out_shape=shapes,
        in_specs=[anywhere] * 5,
        out_specs=[anywhere] * 2,
        scratch_shapes=[
            pltpu.VMEM((2, early) + square, jnp.bfloat16),
            pltpu.VMEM((2, count) + square, jnp.bfloat16),
            pltpu.VMEM((count, 2) + square, jnp.bfloat16),
            pltpu.VMEM((2, count) + square, jnp.bfloat16),
            dma((2, 2)), dma((2,)), dma((2,)), dma((2,)),
        ],
        compiler_params=pltpu.CompilerParams(vmem_limit_bytes=GRANT),
    )(*made, green_real, green_imag)


def solution(mesh):
    blocks = P("kz", "en", None, None)
    counts = (mesh.shape["kz"], mesh.shape["en"])
    return jax.shard_map(
        functools.partial(shards, counts), mesh=mesh,
        in_specs=(blocks, blocks, P(None, None, "kz", None, None), P(), P()),
        out_specs=(blocks, blocks), check_vma=False)
```
